32 devices in a mesh: dom: 8 (over y, x, core), sub: 4 (over z).
Axes of the slice: x: 2, y: 2, z: 4, core: 2. Of those that a mesh axis runs over, the one named last changes fastest.
Arguments:
- upstream: bfloat16 [65536, 128], P(('dom', 'sub')), may hold values from -6 to 6
- features: bfloat16 [65536, 128], P(('dom', 'sub')), may hold values from -6 to 6
- w_in: bfloat16 [128, 128], replicated, may hold values from -0.5 to 0.5
- w_out: bfloat16 [128, 128], replicated, may hold values from -0.5 to 0.5
- inner_adj: bfloat16 [65536, 2048], P(('dom', 'sub')), may hold values from -0.125 to 0.125
- cut_tiles: bfloat16 [768, 128, 128], P(('dom', 'sub')), may hold values from -0.15625 to 0.15625
- cut_list: int32 [768, 3], P(('dom', 'sub')), may hold values from 0 to 511, as said below
- cut_count: int32 [32], P(('dom', 'sub')), may hold values from 1 to 24, as said below
Outputs:
- input_grad: bfloat16 [65536, 128], P(('dom', 'sub'))
- grad_w_in: float32 [128, 128], replicated
- grad_w_out: float32 [128, 128], replicated
The draws below stay inside these ranges and needn't reach their ends.
Inputs may be any that keep to these rules, and one draw needn't show every extreme that they name: `cut_list`: device s's list has 24 rows; column 0 is a local block below 16, column 1 a global block whose device is not s, column 2 a tile id below 24, all tile ids of one device distinct. Among the first cut_count[s] rows the devices of column 1 are all distinct, so one device sends at most one block to another. `cut_count`: some device has exactly 24 live entries in every draw.
All inputs are finite; a program needn't handle non-finite values.
Results may differ from the reference program's by a relative error of at most 0.015.
Values may be sent and summed in bfloat16 or wider, within the bound.
A program may use at most 128 MiB of HBM per device.

```python
import math
import jax
import jax.numpy as jnp
from jax import lax

NB = 16
BLK = 128
EMB = 128
FEAT = 128
HID = 128
STEPS = 4
CMAX = 24
ROWS = 65536
N_DOM = 8
N_SUB = 4


def draw_cut_count(key, part):
    device_count = N_DOM * N_SUB
    key_base, key_heavy, key_pick = jax.random.split(jax.random.fold_in(key, 11), 3)
    base = jax.random.randint(key_base, (device_count,), 1, CMAX // 2 + 1)
    heavy = jax.random.randint(key_heavy, (device_count,), 0, 8) == 0
    picked = jax.random.randint(key_pick, (), 0, device_count)
    heavy = heavy | (jnp.arange(device_count) == picked)
    return jnp.where(heavy, CMAX, base).astype(jnp.int32)


def draw_cut_list(key, part):
    device_count = N_DOM * N_SUB
    list_key = jax.random.fold_in(key, 23)

    def draw_device(device):
        device_key = jax.random.fold_in(list_key, device)
        key_perm, key_target, key_read, key_tile = jax.random.split(device_key, 4)
        shuffled = jax.random.permutation(key_perm, device_count - 1)
        others = shuffled + (shuffled >= device).astype(shuffled.dtype)
        target_dev = others[:CMAX]
        target_block = target_dev * NB + jax.random.randint(key_target, (CMAX,), 0, NB)
        read_block = jax.random.randint(key_read, (CMAX,), 0, NB)
        tile_ids = jax.random.permutation(key_tile, CMAX)
        return jnp.stack([read_block.astype(jnp.int32), target_block.astype(jnp.int32), tile_ids.astype(jnp.int32)], 1)
    stacked = jax.vmap(draw_device)(jnp.arange(device_count, dtype=jnp.int32))
    return stacked.reshape(device_count * CMAX, 3).astype(jnp.int32)


def block_scale(rng, shape, cuts, smallest, top_value):
    def one(dim, blocks):
        steps = jax.random.uniform(jax.random.fold_in(jax.random.fold_in(rng, 6), dim), (blocks,), jnp.float32, smallest / len(cuts), top_value / len(cuts))
        return jnp.repeat(jnp.exp(steps), shape[dim] // blocks).reshape((-1,) + (1,) * (len(shape) - dim - 1))

    loudness = one(*cuts[0])
    for cut in cuts[1:]:
        loudness = loudness * one(*cut)
    return loudness


def noise(stream_key, extent, width, reach, cuts=(), kind=jnp.bfloat16):
    factor_of = block_scale(stream_key, extent, cuts, -0.22, 0.18) if cuts else 1.0
    values = jax.random.normal(stream_key, extent, jnp.float32) * width * factor_of
    return jnp.minimum(jnp.maximum(values, -reach), reach).astype(kind)


def setup_inputs(seed: int = 0) -> dict:
    key_list = jax.random.split(jax.random.key(seed), 9)
    upstream = noise(key_list[0], (ROWS, EMB), 1.0, 6.0, ((0, 32),))
    features = noise(key_list[1], (ROWS, FEAT), 1.0, 6.0, ((0, 32),))
    w_in = noise(key_list[2], (FEAT, HID), FEAT ** -0.5, 0.5)
    w_out = noise(key_list[3], (HID, EMB), HID ** -0.5, 0.5)
    inner_adj = noise(key_list[4], (ROWS, NB * BLK), (NB * BLK) ** -0.5, 0.125, ((0, 32),))
    cut_tiles = noise(key_list[5], (N_DOM * N_SUB * CMAX, BLK, BLK), (BLK * CMAX // 2) ** -0.5, 0.15625, ((0, 32),))
    cut_list = draw_cut_list(jax.random.fold_in(key_list[8], 71), 0)
    cut_count = draw_cut_count(jax.random.fold_in(key_list[8], 71), 0)
    return dict(upstream=upstream, features=features, w_in=w_in, w_out=w_out, inner_adj=inner_adj, cut_tiles=cut_tiles, cut_list=cut_list, cut_count=cut_count)


teleport = 0.1

def reference(upstream, features, w_in, w_out, inner_adj, cut_tiles, cut_list, cut_count):
    device_count = N_DOM * N_SUB
    local_rows = NB * BLK
    total_rows = local_rows * device_count
    adj_blocks = inner_adj.reshape(device_count, local_rows, local_rows)
    tile_sets = cut_tiles.reshape(device_count, CMAX, BLK, BLK)
    list_sets = cut_list.reshape(device_count, CMAX, 3)
    positions = jnp.arange(CMAX, dtype=jnp.int32)

    def local_product(pair):
        return jnp.dot(pair[0], pair[1], preferred_element_type=jnp.float32)

    def propagate(vector):
        parts = vector.reshape(device_count, local_rows, EMB)
        local_terms = lax.map(local_product, (adj_blocks, parts))
        blocks = parts.reshape(device_count, NB, BLK, EMB)

        def sender(carry, inputs):
            tiles_here, list_here, count_here, blocks_here = inputs
            chosen_tiles = tiles_here[list_here[:, 2].astype(jnp.int32)].astype(jnp.float32)
            chosen_blocks = blocks_here[list_here[:, 0].astype(jnp.int32)].astype(jnp.float32)
            products = jnp.einsum('cij,cjk->cik', chosen_tiles, chosen_blocks)
            products = jnp.where((positions < count_here)[:, None, None], products, jnp.zeros_like(products))
            rounded = lax.optimization_barrier(products.astype(jnp.bfloat16))
            carry = carry.at[list_here[:, 1].astype(jnp.int32)].add(rounded.astype(jnp.float32))
            return (carry, None)
        start_sum = jnp.zeros((device_count * NB, BLK, EMB), jnp.float32)
        cut_total, _ = lax.scan(sender, start_sum, (tile_sets, list_sets, cut_count, blocks))
        summed = local_terms.reshape(total_rows, EMB) + cut_total.reshape(total_rows, EMB)
        return ((1.0 - teleport) * summed).astype(jnp.bfloat16)
    vector = upstream
    accum = jnp.zeros((total_rows, EMB), jnp.float32)
    for section_index in range(STEPS):
        accum = accum + teleport * vector.astype(jnp.float32)
        vector = propagate(vector)
    head_grad = (accum + vector.astype(jnp.float32)).astype(jnp.bfloat16)
    pre = jnp.dot(features, w_in, preferred_element_type=jnp.float32)
    gate = jax.nn.sigmoid(pre)
    act = (pre * gate).astype(jnp.bfloat16)
    norm_scale = 1.0 / math.sqrt(total_rows)
    grad_w_out = jnp.einsum('rh,re->he', act.astype(jnp.float32), head_grad.astype(jnp.float32)) * norm_scale
    back = jnp.dot(head_grad, w_out.T, preferred_element_type=jnp.float32)
    dpre = (back * gate * (1.0 + pre * (1.0 - gate))).astype(jnp.bfloat16)
    grad_w_in = jnp.einsum('rf,rh->fh', features.astype(jnp.float32), dpre.astype(jnp.float32)) * norm_scale
    input_grad = jnp.dot(dpre, w_in.T, preferred_element_type=jnp.float32).astype(jnp.bfloat16)
    return (input_grad, grad_w_in, grad_w_out)
```

```python
import functools
import math

import jax
import jax.numpy as jnp
from jax import lax
from jax.experimental import pallas as pl
from jax.experimental.pallas import tpu as pltpu
from jax.sharding import PartitionSpec as P

STEPS = 4
teleport = 0.1
MESH = pl.DeviceIdType.MESH
F32 = jnp.float32
BF16 = jnp.bfloat16
I32 = jnp.int32


def nt_dot(a, b):
    return lax.dot_general(a, b, (((1,), (1,)), ((), ())), preferred_element_type=F32)


def nn_dot(a, b):
    return jnp.dot(a, b, preferred_element_type=F32)


def owner_layout(n_dom, n_sub, grad_rows):
    low = n_sub // 4
    width = n_sub - 2 * low
    chunk = max(8, grad_rows // (n_dom * width))
    return low, width, grad_rows // chunk, chunk


def kernel(
    n_dom, n_sub, norm_scale,
    list_hbm, count_hbm, up_hbm, tiles_hbm, w_in_hbm, w_out_hbm, adj_hbm, feat_hbm,
    dpre_hbm, gfull,
    list_v, count_s, idx_v, idx_s, tiles, w_in, w_out,
    adj, feat, v, outb, arrived, ids_out, ids_in, acc, accum, fac, act_t, feat_t, dpre,
    gsend, gparts, gred,
    local_sem, send_sem, recv_sem, id_send, id_recv, part_send, part_recv, sum_send, sum_recv,
):
    n = n_dom * n_sub
    my_dom, my_sub = lax.axis_index("dom"), lax.axis_index("sub")
    me = my_dom * n_sub + my_sub
    nb, blk, width = v.shape
    rows = nb * blk
    feats, hid = w_in.shape
    tile = min(512, rows)
    blocks = tile // blk
    paired = n_sub & (n_sub - 1) == 0
    pairings = list(reversed(range(n_sub)))
    early = pairings[: n_sub // 2] if n_sub > 1 else []
    arrivals = [(0, 1, n_dom)]
    for m in pairings[:-1]:
        arrivals += [(m, i, min(i + 2, n_dom)) for i in range(0, n_dom, 2)] if m == 1 else [(m, 0, n_dom // 2), (m, n_dom // 2, n_dom)]

    def partner(m, sign):
        if not paired:
            return lax.rem(my_sub + sign * m + n_sub, n_sub)
        z, bit = my_sub, 1
        while bit < n_sub:
            if m & bit:
                z = z + bit - 2 * bit * lax.rem(my_sub // bit, 2)
            bit *= 2
        return z

    def peer(m, i, sign=1):
        d = lax.rem(my_dom + sign * i + n_dom, n_dom)
        z = partner(m, sign)
        return d, z, d * n_sub + z

    def each_peer(fn, chosen=None):
        for m in pairings if chosen is None else chosen:
            def body(i, carry, m=m):
                fn(*peer(m, i))
                return carry
            lax.fori_loop(1 if m == 0 else 0, n_dom, body, 0, unroll=m != 0)

    barrier = pltpu.get_barrier_semaphore()
    each_peer(lambda d, z, t: pl.semaphore_signal(
        barrier, inc=1, device_id=(d, z), device_id_type=MESH))

    loads = [
        pltpu.make_async_copy(src, dst, local_sem.at[i])
        for i, (src, dst) in enumerate([
            (list_hbm, list_v), (count_hbm, count_s), (up_hbm, v), (tiles_hbm, tiles),
            (w_in_hbm, w_in), (w_out_hbm, w_out), (feat_hbm, feat), (adj_hbm, adj)])
    ]
    for load in loads:
        load.start()
    list_load, count_load, up_load, tiles_load, w_in_load, w_out_load, feat_load, adj_load = loads
    list_load.wait()
    count_load.wait()

    entries = list_v.shape[1]
    lanes = idx_v.shape[1]
    first = lax.broadcasted_iota(I32, (n, entries), 0) * nb
    goal = jnp.broadcast_to(list_v[1:2, :], (n, entries))
    live = lax.broadcasted_iota(I32, (n, entries), 1) < count_s[0]
    hit = live & (goal >= first) & (goal < first + nb)

    def pick(values):
        return jnp.sum(jnp.where(hit, values, 0), axis=1, keepdims=True)

    on_diagonal = lax.broadcasted_iota(I32, (n, lanes), 0) == lax.broadcasted_iota(I32, (n, lanes), 1)

    def as_row(column):
        return jnp.sum(jnp.where(on_diagonal, column, 0), axis=0, keepdims=True)

    idx_v[0:1, :] = as_row(pick(list_v[0:1, :]))
    idx_v[1:2, :] = as_row(pick(list_v[2:3, :]))
    idx_copy = pltpu.make_async_copy(idx_v, idx_s, local_sem.at[0])
    idx_copy.start()
    block_id = pick(goal - first - nb) + nb
    ids_out[...] = jnp.broadcast_to(block_id, (n, 128)).reshape(n, 1, 128)
    accum[...] = jnp.zeros_like(accum)

    def id_copy(d, z, t, slot):
        return pltpu.make_async_remote_copy(
            src_ref=ids_out.at[t], dst_ref=ids_in.at[slot], send_sem=id_send.at[t],
            recv_sem=id_recv.at[slot], device_id=(d, z), device_id_type=MESH)

    def block_copy(p, d, z, t, slot):
        return pltpu.make_async_remote_copy(
            src_ref=outb.at[p, t], dst_ref=arrived.at[p, slot], send_sem=send_sem.at[p, t],
            recv_sem=recv_sem.at[p, slot], device_id=(d, z), device_id_type=MESH)

    def multiply(p, t):
        outb[p, t] = nn_dot(tiles[idx_s[1, t]], v[idx_s[0, t]]).astype(BF16)

    idx_copy.wait()
    up_load.wait()
    tiles_load.wait()
    each_peer(lambda d, z, t: multiply(0, t), early)
    pl.semaphore_wait(barrier, n - 1)

    def send_early(d, z, t):
        id_copy(d, z, t, me).start()
        block_copy(0, d, z, t, me).start()

    each_peer(send_early, early)
    late = [m for m in pairings if m not in early]

    for step in range(STEPS):
        p = step % 2

        def send(d, z, t):
            if step >= 2:
                block_copy(p, d, z, t, t).wait_send()
            if step == 0:
                id_copy(d, z, t, me).start()
            multiply(p, t)
            block_copy(p, d, z, t, me).start()

        each_peer(send, late if step == 0 else pairings)

        if step == 0:
            feat_load.wait()
            w_in_load.wait()
            w_out_load.wait()

            def head(i, carry):
                at = pl.ds(pl.multiple_of(i * tile, tile), tile)
                here = feat[at, :]
                pre = nn_dot(here, w_in[...])
                gate = jax.nn.sigmoid(pre)
                act_t[:, at] = (pre * gate).astype(BF16).T
                feat_t[:, at] = here.T
                fac[at, :] = gate * (1.0 + pre * (1.0 - gate))
                return carry

            lax.fori_loop(0, rows // tile, head, 0)
            adj_load.wait()

        def local(i, carry):
            at = pl.ds(pl.multiple_of(i * tile, tile), tile)
            term = nn_dot(adj[at, :], v[...].reshape(rows, width))
            ats = pl.ds(i * blocks, blocks)
            acc[ats] = term.reshape(blocks, blk, width)
            accum[ats] += teleport * v[ats].astype(F32)
            return carry

        lax.fori_loop(0, rows // tile, local, 0)

        for m, start, end in arrivals:
            last = (m, start, end) == arrivals[-1]

            def arrive(i, carry):
                d, z, s = peer(m, i, -1)
                if step == 0:
                    id_copy(d, z, s, s).wait_recv()
                block_copy(p, d, z, s, s).wait_recv()
                return carry

            lax.fori_loop(start, end, arrive, 0)

            def gather(b, carry):
                total = acc[b]
                for i in range(start, end):
                    s = peer(m, i, -1)[2]
                    match = ids_in[s, 0:1, :] == b
                    total += jnp.where(match, arrived[p, s].astype(F32), 0.0)
                if last:
                    v[b] = ((1.0 - teleport) * total).astype(BF16)
                else:
                    acc[b] = total
                return carry

            lax.fori_loop(0, nb, gather, 0, unroll=4)

    def tail(i, carry):
        part_in, part_out = carry
        at = pl.ds(pl.multiple_of(i * tile, tile), tile)
        ats = pl.ds(i * blocks, blocks)
        grad = (accum[ats] + v[ats].astype(F32)).astype(BF16).reshape(tile, width)
        part_out += nn_dot(act_t[:, at], grad)
        back = nt_dot(grad, w_out[...])
        inner = (back * fac[at, :]).astype(BF16)
        dpre[at, :] = inner
        part_in += nn_dot(feat_t[:, at], inner)
        return part_in, part_out

    part_in, part_out = lax.fori_loop(
        0, rows // tile, tail,
        (jnp.zeros((feats, hid), F32), jnp.zeros((hid, width), F32)))
    low, mid, owners, chunk = owner_layout(n_dom, n_sub, feats + hid)
    split = feats // chunk
    gsend[0:split] = (part_in * norm_scale).reshape(split, chunk, hid).astype(BF16)
    gsend[split:owners] = (part_out * norm_scale).reshape(owners - split, chunk, width).astype(BF16)

    def each_owner(fn):
        for j in range(mid):
            def body(i, carry, j=j):
                d = lax.rem(my_dom + i, n_dom)
                q = d * mid + j
                fit = q < owners if n_dom * mid > owners else None
                other = (i > 0) | (my_sub != low + j)
                pl.when(other if fit is None else other & fit)(lambda: fn(d, low + j, q))
                return carry
            lax.fori_loop(0, n_dom, body, 0)

    my_chunk = my_dom * mid + my_sub - low
    owning = (my_sub >= low) & (my_sub < low + mid)
    if n_dom * mid > owners:
        owning = owning & (my_chunk < owners)

    def part_copy(d, z, q, slot):
        return pltpu.make_async_remote_copy(
            src_ref=gsend.at[q], dst_ref=gparts.at[slot], send_sem=part_send.at[q],
            recv_sem=part_recv.at[slot], device_id=(d, z), device_id_type=MESH)

    def sum_copy(d, z, t, q):
        return pltpu.make_async_remote_copy(
            src_ref=gred, dst_ref=gfull.at[q], send_sem=sum_send.at[t],
            recv_sem=sum_recv.at[q], device_id=(d, z), device_id_type=MESH)

    each_owner(lambda d, z, q: part_copy(d, z, q, me).start())
    dpre_copy = pltpu.make_async_copy(dpre, dpre_hbm, local_sem.at[0])
    dpre_copy.start()

    def wait_sends(d, z, t):
        id_copy(d, z, t, t).wait_send()
        block_copy(0, d, z, t, t).wait_send()
        block_copy(1, d, z, t, t).wait_send()

    each_peer(wait_sends)

    def reduce():
        gparts[me] = gsend[my_chunk]
        each_peer(lambda d, z, s: part_copy(d, z, 0, s).wait_recv())
        total = jnp.sum(gparts[...].astype(F32), axis=0).astype(BF16)
        gred[...] = total
        gfull[my_chunk] = total
        each_peer(lambda d, z, t: sum_copy(d, z, t, my_chunk).start())

    pl.when(owning)(reduce)
    each_owner(lambda d, z, q: part_copy(d, z, q, me).wait_send())
    each_owner(lambda d, z, q: sum_copy(d, z, 0, q).wait_recv())
    pl.when(owning)(lambda: each_peer(lambda d, z, t: sum_copy(d, z, t, my_chunk).wait_send()))
    dpre_copy.wait()


def finish(dpre_ref, w_in_ref, gfull_ref, ig_hbm, gin_hbm, gout_hbm, ig, gin, gout, sems):
    owners, chunk, _ = gfull_ref.shape
    split = gin.shape[0] // chunk
    rows = ig.shape[0]
    pieces = 4 if rows % 64 == 0 else 1
    size = rows // pieces
    gin[...] = gfull_ref[0:split].astype(F32).reshape(gin.shape)
    gout[...] = gfull_ref[split:owners].astype(F32).reshape(gout.shape)
    copies = [pltpu.make_async_copy(gin, gin_hbm, sems.at[0]), pltpu.make_async_copy(gout, gout_hbm, sems.at[1])]
    copies[0].start()
    copies[1].start()
    for i in range(pieces):
        at = pl.ds(i * size, size)
        ig[at, :] = nt_dot(dpre_ref[at, :], w_in_ref[...]).astype(BF16)
        copies.append(pltpu.make_async_copy(ig.at[at, :], ig_hbm.at[at, :], sems.at[2 + i]))
        copies[-1].start()
    for copy in copies:
        copy.wait()


def on_device(n_dom, n_sub, upstream, features, w_in, w_out, inner_adj, cut_tiles, cut_list, cut_count):
    n = n_dom * n_sub
    rows, width = upstream.shape
    entries, blk, _ = cut_tiles.shape
    nb = rows // blk
    feats, hid = w_in.shape
    _, _, owners, chunk = owner_layout(n_dom, n_sub, feats + hid)
    lanes = 128 * -(-n // 128)
    vmem = pl.BlockSpec(memory_space=pltpu.VMEM)
    hbm = pl.BlockSpec(memory_space=pl.ANY)
    scratch = [
        pltpu.VMEM((3, entries), I32),
        pltpu.SMEM((1,), I32),
        pltpu.VMEM((2, lanes), I32),
        pltpu.SMEM((2, lanes), I32),
        pltpu.VMEM(cut_tiles.shape, BF16),
        pltpu.VMEM(w_in.shape, BF16),
        pltpu.VMEM(w_out.shape, BF16),
        pltpu.VMEM(inner_adj.shape, BF16),
        pltpu.VMEM(features.shape, BF16),
        pltpu.VMEM((nb, blk, width), BF16),
        pltpu.VMEM((2, n, blk, width), BF16),
        pltpu.VMEM((2, n, blk, width), BF16),
        pltpu.VMEM((n, 1, 128), I32),
        pltpu.VMEM((n, 1, 128), I32),
        pltpu.VMEM((nb, blk, width), F32),
        pltpu.VMEM((nb, blk, width), F32),
        pltpu.VMEM((rows, hid), F32),
        pltpu.VMEM((hid, rows), BF16),
        pltpu.VMEM((feats, rows), BF16),
        pltpu.VMEM((rows, hid), BF16),
        pltpu.VMEM((owners, chunk, hid), BF16),
        pltpu.VMEM((n, chunk, hid), BF16),
        pltpu.VMEM((chunk, hid), BF16),
        pltpu.SemaphoreType.DMA((8,)),
        pltpu.SemaphoreType.DMA((2, n)),
        pltpu.SemaphoreType.DMA((2, n)),
        pltpu.SemaphoreType.DMA((n,)),
        pltpu.SemaphoreType.DMA((n,)),
        pltpu.SemaphoreType.DMA((owners,)),
        pltpu.SemaphoreType.DMA((n,)),
        pltpu.SemaphoreType.DMA((n,)),
        pltpu.SemaphoreType.DMA((owners,)),
    ]
    dpre, sums = pl.pallas_call(
        functools.partial(kernel, n_dom, n_sub, 1.0 / math.sqrt(rows * n)),
        out_shape=(
            jax.ShapeDtypeStruct((rows, hid), BF16),
            jax.ShapeDtypeStruct((owners, chunk, hid), BF16),
        ),
        in_specs=[hbm] * 8,
        out_specs=(hbm, vmem),
        scratch_shapes=scratch,
        compiler_params=pltpu.CompilerParams(collective_id=0, has_side_effects=True),
    )(cut_list.T, cut_count, upstream.reshape(nb, blk, width), cut_tiles, w_in, w_out, inner_adj, features)
    return pl.pallas_call(
        finish,
        out_shape=(
            jax.ShapeDtypeStruct((rows, feats), BF16),
            jax.ShapeDtypeStruct((feats, hid), F32),
            jax.ShapeDtypeStruct((hid, width), F32),
        ),
        in_specs=[vmem] * 3,
        out_specs=(hbm, hbm, hbm),
        scratch_shapes=[
            pltpu.VMEM((rows, feats), BF16),
            pltpu.VMEM((feats, hid), F32),
            pltpu.VMEM((hid, width), F32),
            pltpu.SemaphoreType.DMA((6,)),
        ],
    )(dpre, w_in, sums)


def solution(mesh):
    both = ("dom", "sub")
    placed = (
        P(both, None),
        P(both, None),
        P(),
        P(),
        P(both, None),
        P(both, None, None),
        P(both, None),
        P(both),
    )
    return jax.shard_map(
        functools.partial(on_device, mesh.shape["dom"], mesh.shape["sub"]),
        mesh=mesh,
        in_specs=placed,
        out_specs=(P(both, None), P(), P()),
        check_vma=False,
    )
```

```python
import functools
import math

import jax
import jax.numpy as jnp
from jax import lax
from jax.experimental import pallas as pl
from jax.experimental.pallas import tpu as pltpu
from jax.sharding import PartitionSpec as P

STEPS = 4
teleport = 0.1
MESH = pl.DeviceIdType.MESH
F32 = jnp.float32
BF16 = jnp.bfloat16
I32 = jnp.int32


def nt_dot(a, b):
    return lax.dot_general(a, b, (((1,), (1,)), ((), ())), preferred_element_type=F32)


def nn_dot(a, b):
    return jnp.dot(a, b, preferred_element_type=F32)


def owner_layout(n_dom, n_sub, grad_rows):
    low = n_sub // 4
    width = n_sub - 2 * low
    chunk = max(8, grad_rows // (n_dom * width))
    return low, width, grad_rows // chunk, chunk


def arrival_groups(n_dom, n_sub):
    half = n_dom // 2
    groups = [[(0, 1, n_dom)]] if n_dom > 1 else []
    for m in reversed(range(3, n_sub)):
        groups += [[(m, 0, half)], [(m, half, n_dom)]] if half else [[(m, 0, n_dom)]]
    left = [m for m in (2, 1) if m < n_sub]
    cuts = sorted({0, half, half + half // 2, n_dom - 1, n_dom})
    for start, end in zip(cuts[:-1], cuts[1:]):
        if end == n_dom:
            groups.append([(m, start, end) for m in left])
        else:
            groups += [[(m, start, end)] for m in left]
    return [group for group in groups if group]


def kernel(
    n_dom, n_sub, norm_scale,
    list_hbm, count_hbm, up_hbm, tiles_hbm, w_in_hbm, w_out_hbm, adj_hbm, feat_hbm,
    ig_hbm, gfull,
    list_v, count_s, idx_v, idx_s, tiles, w_in, w_out,
    adj, feat, v, outb, arrived, ids_out, ids_in, acc, accum, fac, act_t, feat_t, dpre, ig,
    gsend, gparts, gred,
    local_sem, send_sem, recv_sem, small_sem,
):
    n = n_dom * n_sub
    my_dom, my_sub = lax.axis_index("dom"), lax.axis_index("sub")
    me = my_dom * n_sub + my_sub
    nb, blk, width = v.shape
    rows = nb * blk
    feats, hid = w_in.shape
    tile = min(512, rows)
    blocks = tile // blk
    paired = n_sub & (n_sub - 1) == 0
    pairings = list(reversed(range(n_sub)))
    early = pairings[: n_sub // 2] if n_sub > 1 else []
    groups = arrival_groups(n_dom, n_sub)
    group_of = {(m, i): k for k, pieces in enumerate(groups) for m, start, end in pieces for i in range(start, end)}

    def partner(m, sign):
        if not paired:
            return lax.rem(my_sub + sign * m + n_sub, n_sub)
        z, bit = my_sub, 1
        while bit < n_sub:
            if m & bit:
                z = z + bit - 2 * bit * lax.rem(my_sub // bit, 2)
            bit *= 2
        return z

    def peer(m, i, sign=1):
        d = lax.rem(my_dom + sign * i + n_dom, n_dom)
        z = partner(m, sign)
        return d, z, d * n_sub + z

    def each_peer(fn, chosen=None):
        for m in pairings if chosen is None else chosen:
            i = 1 if m == 0 else 0
            while i < n_dom:
                k = group_of[m, i]
                end = i
                while end < n_dom and group_of[m, end] == k:
                    end += 1
                def body(i, carry, m=m, k=k):
                    fn(*peer(m, i), k)
                    return carry
                lax.fori_loop(i, end, body, 0, unroll=m != 0)
                i = end

    barrier = pltpu.get_barrier_semaphore()
    each_peer(lambda d, z, t, k: pl.semaphore_signal(
        barrier, inc=1, device_id=(d, z), device_id_type=MESH))

    loads = [
        pltpu.make_async_copy(src, dst, local_sem.at[i])
        for i, (src, dst) in enumerate([
            (list_hbm, list_v), (count_hbm, count_s), (up_hbm, v), (tiles_hbm, tiles),
            (w_in_hbm, w_in), (w_out_hbm, w_out), (feat_hbm, feat), (adj_hbm, adj)])
    ]
    for load in loads:
        load.start()
    list_load, count_load, up_load, tiles_load, w_in_load, w_out_load, feat_load, adj_load = loads
    list_load.wait()
    count_load.wait()

    entries = list_v.shape[1]
    lanes = idx_v.shape[1]
    first = lax.broadcasted_iota(I32, (n, entries), 0) * nb
    goal = jnp.broadcast_to(list_v[1:2, :], (n, entries))
    live = lax.broadcasted_iota(I32, (n, entries), 1) < count_s[0]
    hit = live & (goal >= first) & (goal < first + nb)

    def pick(values):
        return jnp.sum(jnp.where(hit, values, 0), axis=1, keepdims=True)

    on_diagonal = lax.broadcasted_iota(I32, (n, lanes), 0) == lax.broadcasted_iota(I32, (n, lanes), 1)

    def as_row(column):
        return jnp.sum(jnp.where(on_diagonal, column, 0), axis=0, keepdims=True)

    idx_v[0:1, :] = as_row(pick(list_v[0:1, :]))
    idx_v[1:2, :] = as_row(pick(list_v[2:3, :]))
    idx_copy = pltpu.make_async_copy(idx_v, idx_s, local_sem.at[0])
    idx_copy.start()
    block_id = pick(goal - first - nb) + nb
    ids_out[...] = jnp.broadcast_to(block_id, (n, 128)).reshape(n, 1, 128)
    accum[...] = jnp.zeros_like(accum)

    def id_copy(d, z, t, slot):
        return pltpu.make_async_remote_copy(
            src_ref=ids_out.at[t], dst_ref=ids_in.at[slot], send_sem=small_sem.at[0],
            recv_sem=small_sem.at[1], device_id=(d, z), device_id_type=MESH)

    def block_copy(p, d, z, t, k):
        return pltpu.make_async_remote_copy(
            src_ref=outb.at[p, t], dst_ref=arrived.at[p, me], send_sem=send_sem.at[p],
            recv_sem=recv_sem.at[p, k], device_id=(d, z), device_id_type=MESH)

    def many(ref, count, sem):
        return pltpu.make_async_remote_copy(
            src_ref=ref.at[pl.ds(0, count)], dst_ref=ref.at[pl.ds(0, count)], send_sem=sem,
            recv_sem=sem, device_id=(my_dom, my_sub), device_id_type=MESH)

    def multiply(p, t):
        outb[p, t] = nn_dot(tiles[idx_s[1, t]], v[idx_s[0, t]]).astype(BF16)

    idx_copy.wait()
    up_load.wait()
    tiles_load.wait()
    each_peer(lambda d, z, t, k: multiply(0, t), early)
    pl.semaphore_wait(barrier, n - 1)

    each_peer(lambda d, z, t, k: id_copy(d, z, t, me).start())
    each_peer(lambda d, z, t, k: block_copy(0, d, z, t, k).start(), early)
    late = [m for m in pairings if m not in early]

    for step in range(STEPS):
        p = step % 2

        def send(d, z, t, k):
            multiply(p, t)
            block_copy(p, d, z, t, k).start()

        if step >= 2:
            many(outb.at[p], n - 1, send_sem.at[p]).wait_send()

        each_peer(send, late if step == 0 else pairings)

        if step == 0:
            feat_load.wait()
            w_in_load.wait()
            w_out_load.wait()

            def head(i, carry):
                at = pl.ds(pl.multiple_of(i * tile, tile), tile)
                here = feat[at, :]
                pre = nn_dot(here, w_in[...])
                gate = jax.nn.sigmoid(pre)
                act_t[:, at] = (pre * gate).astype(BF16).T
                feat_t[:, at] = here.T
                fac[at, :] = gate * (1.0 + pre * (1.0 - gate))
                return carry

            lax.fori_loop(0, rows // tile, head, 0)
            adj_load.wait()

        def local(i, carry):
            at = pl.ds(pl.multiple_of(i * tile, tile), tile)
            term = nn_dot(adj[at, :], v[...].reshape(rows, width))
            ats = pl.ds(i * blocks, blocks)
            acc[ats] = term.reshape(blocks, blk, width)
            accum[ats] += teleport * v[ats].astype(F32)
            return carry

        lax.fori_loop(0, rows // tile, local, 0)

        for k, pieces in enumerate(groups):
            last = k == len(groups) - 1
            if step == 0 and k == 0:
                many(ids_in, n - 1, small_sem.at[1]).wait_recv()
            count = sum(end - start for _, start, end in pieces)
            many(arrived.at[p], count, recv_sem.at[p, k]).wait_recv()

            def gather(b, carry):
                total = acc[b]
                for m, start, end in pieces:
                    for i in range(start, end):
                        s = peer(m, i, -1)[2]
                        match = ids_in[s, 0:1, :] == b
                        total += jnp.where(match, arrived[p, s].astype(F32), 0.0)
                if last:
                    v[b] = ((1.0 - teleport) * total).astype(BF16)
                else:
                    acc[b] = total
                return carry

            lax.fori_loop(0, nb, gather, 0, unroll=4)

    def tail(i, carry):
        part_in, part_out = carry
        at = pl.ds(pl.multiple_of(i * tile, tile), tile)
        ats = pl.ds(i * blocks, blocks)
        grad = (accum[ats] + v[ats].astype(F32)).astype(BF16).reshape(tile, width)
        part_out += nn_dot(act_t[:, at], grad)
        back = nt_dot(grad, w_out[...])
        inner = (back * fac[at, :]).astype(BF16)
        dpre[at, :] = inner
        part_in += nn_dot(feat_t[:, at], inner)
        return part_in, part_out

    part_in, part_out = lax.fori_loop(
        0, rows // tile, tail,
        (jnp.zeros((feats, hid), F32), jnp.zeros((hid, width), F32)), unroll=True)
    low, mid, owners, chunk = owner_layout(n_dom, n_sub, feats + hid)
    split = feats // chunk
    gsend[0:split] = (part_in * norm_scale).reshape(split, chunk, hid).astype(BF16)
    gsend[split:owners] = (part_out * norm_scale).reshape(owners - split, chunk, width).astype(BF16)

    def each_owner(fn):
        for j in range(mid):
            def body(i, carry, j=j):
                d = lax.rem(my_dom + i, n_dom)
                q = d * mid + j
                fit = q < owners if n_dom * mid > owners else None
                other = (i > 0) | (my_sub != low + j)
                pl.when(other if fit is None else other & fit)(lambda: fn(d, low + j, q))
                return carry
            lax.fori_loop(0, n_dom, body, 0)

    my_chunk = my_dom * mid + my_sub - low
    owning = (my_sub >= low) & (my_sub < low + mid)
    if n_dom * mid > owners:
        owning = owning & (my_chunk < owners)

    def part_copy(d, z, q, slot):
        return pltpu.make_async_remote_copy(
            src_ref=gsend.at[q], dst_ref=gparts.at[slot], send_sem=small_sem.at[2],
            recv_sem=small_sem.at[3], device_id=(d, z), device_id_type=MESH)

    def sum_copy(d, z, q):
        return pltpu.make_async_remote_copy(
            src_ref=gred, dst_ref=gfull.at[q], send_sem=small_sem.at[4],
            recv_sem=small_sem.at[5], device_id=(d, z), device_id_type=MESH)

    each_owner(lambda d, z, q: part_copy(d, z, q, me).start())

    def project(i, carry):
        at = pl.ds(pl.multiple_of(i * tile, tile), tile)
        ig[at, :] = nt_dot(dpre[at, :], w_in[...]).astype(BF16)
        return carry

    lax.fori_loop(0, rows // tile, project, 0)
    ig_copy = pltpu.make_async_copy(ig, ig_hbm, local_sem.at[0])
    ig_copy.start()
    many(ids_out, n - 1, small_sem.at[0]).wait_send()
    many(outb.at[0], n - 1, send_sem.at[0]).wait_send()
    many(outb.at[1], n - 1, send_sem.at[1]).wait_send()

    def reduce():
        gparts[me] = gsend[my_chunk]
        many(gparts, n - 1, small_sem.at[3]).wait_recv()
        total = jnp.sum(gparts[...].astype(F32), axis=0).astype(BF16)
        gred[...] = total
        gfull[my_chunk] = total
        each_peer(lambda d, z, t, k: sum_copy(d, z, my_chunk).start())
        many(gsend, owners - 1, small_sem.at[2]).wait_send()
        many(gfull, owners - 1, small_sem.at[5]).wait_recv()
        many(gparts, n - 1, small_sem.at[4]).wait_send()

    def follow():
        many(gsend, owners, small_sem.at[2]).wait_send()
        many(gfull, owners, small_sem.at[5]).wait_recv()

    pl.when(owning)(reduce)
    pl.when(jnp.logical_not(owning))(follow)
    ig_copy.wait()


PIECES = 4


def finish(ig_in, sums_in, ig_out, gin_out, gout_out, ig, sums, gin, gout, sems):
    owners, chunk, _ = sums.shape
    split = gin.shape[0] // chunk
    size = ig.shape[0] // PIECES
    pieces = [pl.ds(i * size, size) for i in range(PIECES)]
    sums_load = pltpu.make_async_copy(sums_in, sums, sems.at[0])
    loads = [pltpu.make_async_copy(ig_in.at[at, :], ig.at[at, :], sems.at[3 + i]) for i, at in enumerate(pieces)]
    stores = [pltpu.make_async_copy(ig.at[at, :], ig_out.at[at, :], sems.at[3 + i]) for i, at in enumerate(pieces)]
    stores += [pltpu.make_async_copy(gin, gin_out, sems.at[1]), pltpu.make_async_copy(gout, gout_out, sems.at[2])]
    sums_load.start()
    for load in loads:
        load.start()
    sums_load.wait()
    gin[...] = sums[0:split].astype(F32).reshape(gin.shape)
    stores[-2].start()
    gout[...] = sums[split:owners].astype(F32).reshape(gout.shape)
    stores[-1].start()
    for load, store in zip(loads, stores):
        load.wait()
        store.start()
    for store in stores:
        store.wait()


def on_device(n_dom, n_sub, upstream, features, w_in, w_out, inner_adj, cut_tiles, cut_list, cut_count):
    n = n_dom * n_sub
    rows, width = upstream.shape
    entries, blk, _ = cut_tiles.shape
    nb = rows // blk
    feats, hid = w_in.shape
    _, _, owners, chunk = owner_layout(n_dom, n_sub, feats + hid)
    lanes = 128 * -(-n // 128)
    vmem = pl.BlockSpec(memory_space=pltpu.VMEM)
    hbm = pl.BlockSpec(memory_space=pl.ANY)
    scratch = [
        pltpu.VMEM((3, entries), I32),
        pltpu.SMEM((1,), I32),
        pltpu.VMEM((2, lanes), I32),
        pltpu.SMEM((2, lanes), I32),
        pltpu.VMEM(cut_tiles.shape, BF16),
        pltpu.VMEM(w_in.shape, BF16),
        pltpu.VMEM(w_out.shape, BF16),
        pltpu.VMEM(inner_adj.shape, BF16),
        pltpu.VMEM(features.shape, BF16),
        pltpu.VMEM((nb, blk, width), BF16),
        pltpu.VMEM((2, n, blk, width), BF16),
        pltpu.VMEM((2, n, blk, width), BF16),
        pltpu.VMEM((n, 1, 128), I32),
        pltpu.VMEM((n, 1, 128), I32),
        pltpu.VMEM((nb, blk, width), F32),
        pltpu.VMEM((nb, blk, width), F32),
        pltpu.VMEM((rows, hid), F32),
        pltpu.VMEM((hid, rows), BF16),
        pltpu.VMEM((feats, rows), BF16),
        pltpu.VMEM((rows, hid), BF16),
        pltpu.VMEM((rows, feats), BF16),
        pltpu.VMEM((owners, chunk, hid), BF16),
        pltpu.VMEM((n, chunk, hid), BF16),
        pltpu.VMEM((chunk, hid), BF16),
        pltpu.SemaphoreType.DMA((8,)),
        pltpu.SemaphoreType.DMA((2,)),
        pltpu.SemaphoreType.DMA((2, len(arrival_groups(n_dom, n_sub)))),
        pltpu.SemaphoreType.DMA((6,)),
    ]
    ig, sums = pl.pallas_call(
        functools.partial(kernel, n_dom, n_sub, 1.0 / math.sqrt(rows * n)),
        out_shape=(
            jax.ShapeDtypeStruct((rows, feats), BF16),
            jax.ShapeDtypeStruct((owners, chunk, hid), BF16),
        ),
        in_specs=[hbm] * 8,
        out_specs=(hbm, vmem),
        scratch_shapes=scratch,
        compiler_params=pltpu.CompilerParams(collective_id=0, has_side_effects=True),
    )(cut_list.T, cut_count, upstream.reshape(nb, blk, width), cut_tiles, w_in, w_out, inner_adj, features)
    return pl.pallas_call(
        finish,
        out_shape=(
            jax.ShapeDtypeStruct((rows, feats), BF16),
            jax.ShapeDtypeStruct((feats, hid), F32),
            jax.ShapeDtypeStruct((hid, width), F32),
        ),
        in_specs=[hbm, hbm],
        out_specs=(hbm, hbm, hbm),
        scratch_shapes=[
            pltpu.VMEM((rows, feats), BF16),
            pltpu.VMEM(sums.shape, BF16),
            pltpu.VMEM((feats, hid), F32),
            pltpu.VMEM((hid, width), F32),
            pltpu.SemaphoreType.DMA((3 + PIECES,)),
        ],
    )(ig, sums)


def solution(mesh):
    both = ("dom", "sub")
    placed = (
        P(both, None),
        P(both, None),
        P(),
        P(),
        P(both, None),
        P(both, None, None),
        P(both, None),
        P(both),
    )
    return jax.shard_map(
        functools.partial(on_device, mesh.shape["dom"], mesh.shape["sub"]),
        mesh=mesh,
        in_specs=placed,
        out_specs=(P(both, None), P(), P()),
        check_vma=False,
    )
```

```python
import functools
import math

import jax
import jax.numpy as jnp
from jax import lax
from jax.experimental import pallas as pl
from jax.experimental.pallas import tpu as pltpu
from jax.sharding import PartitionSpec as P

STEPS = 4
teleport = 0.1
MESH = pl.DeviceIdType.MESH
F32 = jnp.float32
BF16 = jnp.bfloat16
I32 = jnp.int32


def nt_dot(a, b):
    return lax.dot_general(a, b, (((1,), (1,)), ((), ())), preferred_element_type=F32)


def nn_dot(a, b):
    return jnp.dot(a, b, preferred_element_type=F32)


def owner_layout(n_dom, n_sub, grad_rows):
    low = n_sub // 4
    width = n_sub - 2 * low
    chunk = max(8, grad_rows // (n_dom * width))
    return low, width, grad_rows // chunk, chunk


def arrival_groups(n_dom, n_sub):
    half = n_dom // 2
    groups = [[(0, 1, n_dom)]] if n_dom > 1 else []
    for m in reversed(range(3, n_sub)):
        groups += [[(m, 0, half)], [(m, half, n_dom)]] if half else [[(m, 0, n_dom)]]
    left = [m for m in (2, 1) if m < n_sub]
    cuts = sorted({0, half, half + half // 2, n_dom - 1, n_dom})
    for start, end in zip(cuts[:-1], cuts[1:]):
        if end == n_dom:
            groups.append([(m, start, end) for m in left])
        else:
            groups += [[(m, start, end)] for m in left]
    return [group for group in groups if group]


def kernel(
    n_dom, n_sub, norm_scale,
    list_hbm, count_hbm, up_hbm, tiles_hbm, w_in_hbm, w_out_hbm, adj_hbm, feat_hbm,
    ig_hbm, gfull,
    list_v, count_s, idx_v, idx_s, tiles, w_in, w_out,
    adj, feat, v, outb, arrived, ids_out, ids_in, acc, accum, fac, act_t, feat_t, dpre, ig,
    gsend, gparts, gred,
    local_sem, send_sem, recv_sem, small_sem,
):
    n = n_dom * n_sub
    my_dom, my_sub = lax.axis_index("dom"), lax.axis_index("sub")
    me = my_dom * n_sub + my_sub
    nb, blk, width = v.shape
    rows = nb * blk
    feats, hid = w_in.shape
    tile = min(512, rows)
    blocks = tile // blk
    paired = n_sub & (n_sub - 1) == 0
    pairings = list(reversed(range(n_sub)))
    early = pairings[: n_sub // 2] if n_sub > 1 else []
    groups = arrival_groups(n_dom, n_sub)
    group_of = {(m, i): k for k, pieces in enumerate(groups) for m, start, end in pieces for i in range(start, end)}

    def partner(m, sign):
        if not paired:
            return lax.rem(my_sub + sign * m + n_sub, n_sub)
        z, bit = my_sub, 1
        while bit < n_sub:
            if m & bit:
                z = z + bit - 2 * bit * lax.rem(my_sub // bit, 2)
            bit *= 2
        return z

    def peer(m, i, sign=1):
        d = lax.rem(my_dom + sign * i + n_dom, n_dom)
        z = partner(m, sign)
        return d, z, d * n_sub + z

    def each_peer(fn, chosen=None):
        for m in pairings if chosen is None else chosen:
            i = 1 if m == 0 else 0
            while i < n_dom:
                k = group_of[m, i]
                end = i
                while end < n_dom and group_of[m, end] == k:
                    end += 1
                def body(i, carry, m=m, k=k):
                    fn(*peer(m, i), k)
                    return carry
                lax.fori_loop(i, end, body, 0, unroll=m != 0)
                i = end

    barrier = pltpu.get_barrier_semaphore()
    each_peer(lambda d, z, t, k: pl.semaphore_signal(
        barrier, inc=1, device_id=(d, z), device_id_type=MESH))

    loads = [
        pltpu.make_async_copy(src, dst, local_sem.at[i])
        for i, (src, dst) in enumerate([
            (list_hbm, list_v), (count_hbm, count_s), (up_hbm, v), (tiles_hbm, tiles),
            (w_in_hbm, w_in), (w_out_hbm, w_out), (feat_hbm, feat), (adj_hbm, adj)])
    ]
    for load in loads:
        load.start()
    list_load, count_load, up_load, tiles_load, w_in_load, w_out_load, feat_load, adj_load = loads
    list_load.wait()
    count_load.wait()

    entries = list_v.shape[1]
    lanes = idx_v.shape[1]
    first = lax.broadcasted_iota(I32, (n, entries), 0) * nb
    goal = jnp.broadcast_to(list_v[1:2, :], (n, entries))
    live = lax.broadcasted_iota(I32, (n, entries), 1) < count_s[0]
    hit = live & (goal >= first) & (goal < first + nb)

    def pick(values):
        return jnp.sum(jnp.where(hit, values, 0), axis=1, keepdims=True)

    on_diagonal = lax.broadcasted_iota(I32, (n, lanes), 0) == lax.broadcasted_iota(I32, (n, lanes), 1)

    def as_row(column):
        return jnp.sum(jnp.where(on_diagonal, column, 0), axis=0, keepdims=True)

    idx_v[0:1, :] = as_row(pick(list_v[0:1, :]))
    idx_v[1:2, :] = as_row(pick(list_v[2:3, :]))
    idx_copy = pltpu.make_async_copy(idx_v, idx_s, local_sem.at[0])
    idx_copy.start()
    block_id = pick(goal - first - nb) + nb
    ids_out[...] = jnp.broadcast_to(block_id, (n, 128)).reshape(n, 1, 128)
    accum[...] = jnp.zeros_like(accum)

    def id_copy(d, z, t, slot):
        return pltpu.make_async_remote_copy(
            src_ref=ids_out.at[t], dst_ref=ids_in.at[slot], send_sem=small_sem.at[0],
            recv_sem=small_sem.at[1], device_id=(d, z), device_id_type=MESH)

    def block_copy(p, d, z, t, k):
        return pltpu.make_async_remote_copy(
            src_ref=outb.at[p, t], dst_ref=arrived.at[p, me], send_sem=send_sem.at[p],
            recv_sem=recv_sem.at[p, k], device_id=(d, z), device_id_type=MESH)

    def many(ref, count, sem):
        return pltpu.make_async_remote_copy(
            src_ref=ref.at[pl.ds(0, count)], dst_ref=ref.at[pl.ds(0, count)], send_sem=sem,
            recv_sem=sem, device_id=(my_dom, my_sub), device_id_type=MESH)

    def multiply(p, t):
        outb[p, t] = nn_dot(tiles[idx_s[1, t]], v[idx_s[0, t]]).astype(BF16)

    idx_copy.wait()
    up_load.wait()
    tiles_load.wait()
    each_peer(lambda d, z, t, k: multiply(0, t), early)
    pl.semaphore_wait(barrier, n - 1)

    each_peer(lambda d, z, t, k: id_copy(d, z, t, me).start())
    each_peer(lambda d, z, t, k: block_copy(0, d, z, t, k).start(), early)
    late = [m for m in pairings if m not in early]

    for step in range(STEPS):
        p = step % 2

        def send(d, z, t, k):
            multiply(p, t)
            block_copy(p, d, z, t, k).start()

        if step >= 2:
            many(outb.at[p], n - 1, send_sem.at[p]).wait_send()

        each_peer(send, late if step == 0 else pairings)

        if step == 0:
            feat_load.wait()
            w_in_load.wait()
            w_out_load.wait()

            def head(i, carry):
                at = pl.ds(pl.multiple_of(i * tile, tile), tile)
                here = feat[at, :]
                pre = nn_dot(here, w_in[...])
                gate = jax.nn.sigmoid(pre)
                act_t[:, at] = (pre * gate).astype(BF16).T
                feat_t[:, at] = here.T
                fac[at, :] = gate * (1.0 + pre * (1.0 - gate))
                return carry

            lax.fori_loop(0, rows // tile, head, 0)
            adj_load.wait()

        def local(i, carry):
            at = pl.ds(pl.multiple_of(i * tile, tile), tile)
            term = nn_dot(adj[at, :], v[...].reshape(rows, width))
            ats = pl.ds(i * blocks, blocks)
            acc[ats] = term.reshape(blocks, blk, width)
            accum[ats] += teleport * v[ats].astype(F32)
            return carry

        lax.fori_loop(0, rows // tile, local, 0)

        for k, pieces in enumerate(groups):
            last = k == len(groups) - 1
            if step == 0 and k == 0:
                many(ids_in, n - 1, small_sem.at[1]).wait_recv()
            count = sum(end - start for _, start, end in pieces)
            many(arrived.at[p], count, recv_sem.at[p, k]).wait_recv()

            def summed(b):
                total = acc[b]
                for m, start, end in pieces:
                    for i in range(start, end):
                        s = peer(m, i, -1)[2]
                        match = ids_in[s, 0:1, :] == b
                        total += jnp.where(match, arrived[p, s].astype(F32), 0.0)
                return total

            def gather(b, carry):
                if last:
                    v[b] = ((1.0 - teleport) * summed(b)).astype(BF16)
                else:
                    acc[b] = summed(b)
                return carry

            if not (last and step == STEPS - 1):
                lax.fori_loop(0, nb, gather, 0, unroll=4)

    def head_grad(b):
        final = ((1.0 - teleport) * summed(b)).astype(BF16)
        return (accum[b] + final.astype(F32)).astype(BF16)

    low, mid, owners, chunk = owner_layout(n_dom, n_sub, feats + hid)
    split = feats // chunk

    def each_owner(fn, wanted=None):
        for k in range(mid):
            j = jnp.where(my_sub < low + (mid + 1) // 2, mid - 1 - k, k)

            def body(i, carry, j=j):
                d = lax.rem(my_dom + i, n_dom)
                q = d * mid + j
                fit = q < owners if n_dom * mid > owners else None
                other = (i > 0) | (my_sub != low + j)
                other = other if fit is None else other & fit
                pl.when(other if wanted is None else other & wanted(q))(lambda: fn(d, low + j, q))
                return carry
            lax.fori_loop(0, n_dom, body, 0)

    my_chunk = my_dom * mid + my_sub - low
    owning = (my_sub >= low) & (my_sub < low + mid)
    if n_dom * mid > owners:
        owning = owning & (my_chunk < owners)

    def part_copy(d, z, q, slot):
        return pltpu.make_async_remote_copy(
            src_ref=gsend.at[q], dst_ref=gparts.at[slot], send_sem=small_sem.at[2],
            recv_sem=small_sem.at[3], device_id=(d, z), device_id_type=MESH)

    def sum_copy(d, z, q):
        return pltpu.make_async_remote_copy(
            src_ref=gred, dst_ref=gfull.at[q], send_sem=small_sem.at[4],
            recv_sem=small_sem.at[5], device_id=(d, z), device_id_type=MESH)

    def tail_out(i, part_out):
        at = pl.ds(pl.multiple_of(i * tile, tile), tile)
        ats = pl.ds(i * blocks, blocks)
        grad = jnp.concatenate([head_grad(i * blocks + j) for j in range(blocks)], axis=0)
        v[ats] = grad.reshape(blocks, blk, width)
        return part_out + nn_dot(act_t[:, at], grad)

    part_out = lax.fori_loop(0, rows // tile, tail_out, jnp.zeros((hid, width), F32), unroll=True)
    gsend[split:owners] = (part_out * norm_scale).reshape(owners - split, chunk, width).astype(BF16)
    each_owner(lambda d, z, q: part_copy(d, z, q, me).start(), lambda q: q >= split)

    def tail_in(i, part_in):
        at = pl.ds(pl.multiple_of(i * tile, tile), tile)
        ats = pl.ds(i * blocks, blocks)
        back = nt_dot(v[ats].reshape(tile, width), w_out[...])
        inner = (back * fac[at, :]).astype(BF16)
        dpre[at, :] = inner
        return part_in + nn_dot(feat_t[:, at], inner)

    part_in = lax.fori_loop(0, rows // tile, tail_in, jnp.zeros((feats, hid), F32), unroll=True)
    gsend[0:split] = (part_in * norm_scale).reshape(split, chunk, hid).astype(BF16)
    each_owner(lambda d, z, q: part_copy(d, z, q, me).start(), lambda q: q < split)

    def project(i, carry):
        at = pl.ds(pl.multiple_of(i * tile, tile), tile)
        ig[at, :] = nt_dot(dpre[at, :], w_in[...]).astype(BF16)
        return carry

    lax.fori_loop(0, rows // tile, project, 0)
    ig_copy = pltpu.make_async_copy(ig, ig_hbm, local_sem.at[0])
    ig_copy.start()
    many(ids_out, n - 1, small_sem.at[0]).wait_send()
    many(outb.at[0], n - 1, send_sem.at[0]).wait_send()
    many(outb.at[1], n - 1, send_sem.at[1]).wait_send()

    def reduce():
        gparts[me] = gsend[my_chunk]
        many(gparts, n - 1, small_sem.at[3]).wait_recv()
        total = jnp.sum(gparts[...].astype(F32), axis=0).astype(BF16)
        gred[...] = total
        mine = pltpu.make_async_copy(gred, gfull.at[my_chunk], local_sem.at[1])
        mine.start()
        each_peer(lambda d, z, t, k: sum_copy(d, z, my_chunk).start())
        many(gsend, owners - 1, small_sem.at[2]).wait_send()
        many(gfull, owners - 1, small_sem.at[5]).wait_recv()
        many(gparts, n - 1, small_sem.at[4]).wait_send()
        mine.wait()

    def follow():
        many(gsend, owners, small_sem.at[2]).wait_send()
        many(gfull, owners, small_sem.at[5]).wait_recv()

    pl.when(owning)(reduce)
    pl.when(jnp.logical_not(owning))(follow)
    ig_copy.wait()


PIECES = 8


def finish(ig_in, sums_in, ig_out, gin_out, gout_out, ig, sums, gin, gout, sems):
    owners, chunk, _ = sums.shape
    split = gin.shape[0] // chunk
    size = ig.shape[0] // PIECES
    pieces = [pl.ds(i * size, size) for i in range(PIECES)]
    sums_load = pltpu.make_async_copy(sums_in, sums, sems.at[0])
    loads = [pltpu.make_async_copy(ig_in.at[at, :], ig.at[at, :], sems.at[3 + i]) for i, at in enumerate(pieces)]
    stores = [pltpu.make_async_copy(ig.at[at, :], ig_out.at[at, :], sems.at[3 + i]) for i, at in enumerate(pieces)]
    stores += [pltpu.make_async_copy(gin, gin_out, sems.at[1]), pltpu.make_async_copy(gout, gout_out, sems.at[2])]
    sums_load.start()
    for load in loads:
        load.start()
    sums_load.wait()
    gin[...] = sums[0:split].astype(F32).reshape(gin.shape)
    stores[-2].start()
    gout[...] = sums[split:owners].astype(F32).reshape(gout.shape)
    stores[-1].start()
    for load, store in zip(loads, stores):
        load.wait()
        store.start()
    for store in stores:
        store.wait()


def on_device(n_dom, n_sub, upstream, features, w_in, w_out, inner_adj, cut_tiles, cut_list, cut_count):
    n = n_dom * n_sub
    rows, width = upstream.shape
    entries, blk, _ = cut_tiles.shape
    nb = rows // blk
    feats, hid = w_in.shape
    _, _, owners, chunk = owner_layout(n_dom, n_sub, feats + hid)
    lanes = 128 * -(-n // 128)
    vmem = pl.BlockSpec(memory_space=pltpu.VMEM)
    hbm = pl.BlockSpec(memory_space=pl.ANY)
    scratch = [
        pltpu.VMEM((3, entries), I32),
        pltpu.SMEM((1,), I32),
        pltpu.VMEM((2, lanes), I32),
        pltpu.SMEM((2, lanes), I32),
        pltpu.VMEM(cut_tiles.shape, BF16),
        pltpu.VMEM(w_in.shape, BF16),
        pltpu.VMEM(w_out.shape, BF16),
        pltpu.VMEM(inner_adj.shape, BF16),
        pltpu.VMEM(features.shape, BF16),
        pltpu.VMEM((nb, blk, width), BF16),
        pltpu.VMEM((2, n, blk, width), BF16),
        pltpu.VMEM((2, n, blk, width), BF16),
        pltpu.VMEM((n, 1, 128), I32),
        pltpu.VMEM((n, 1, 128), I32),
        pltpu.VMEM((nb, blk, width), F32),
        pltpu.VMEM((nb, blk, width), F32),
        pltpu.VMEM((rows, hid), F32),
        pltpu.VMEM((hid, rows), BF16),
        pltpu.VMEM((feats, rows), BF16),
        pltpu.VMEM((rows, hid), BF16),
        pltpu.VMEM((rows, feats), BF16),
        pltpu.VMEM((owners, chunk, hid), BF16),
        pltpu.VMEM((n, chunk, hid), BF16),
        pltpu.VMEM((chunk, hid), BF16),
        pltpu.SemaphoreType.DMA((8,)),
        pltpu.SemaphoreType.DMA((2,)),
        pltpu.SemaphoreType.DMA((2, len(arrival_groups(n_dom, n_sub)))),
        pltpu.SemaphoreType.DMA((6,)),
    ]
    ig, sums = pl.pallas_call(
        functools.partial(kernel, n_dom, n_sub, 1.0 / math.sqrt(rows * n)),
        out_shape=(
            jax.ShapeDtypeStruct((rows, feats), BF16),
            jax.ShapeDtypeStruct((owners, chunk, hid), BF16),
        ),
        in_specs=[hbm] * 8,
        out_specs=(hbm, hbm),
        scratch_shapes=scratch,
        compiler_params=pltpu.CompilerParams(collective_id=0, has_side_effects=True),
    )(cut_list.T, cut_count, upstream.reshape(nb, blk, width), cut_tiles, w_in, w_out, inner_adj, features)
    return pl.pallas_call(
        finish,
        out_shape=(
            jax.ShapeDtypeStruct((rows, feats), BF16),
            jax.ShapeDtypeStruct((feats, hid), F32),
            jax.ShapeDtypeStruct((hid, width), F32),
        ),
        in_specs=[hbm, hbm],
        out_specs=(hbm, hbm, hbm),
        scratch_shapes=[
            pltpu.VMEM((rows, feats), BF16),
            pltpu.VMEM(sums.shape, BF16),
            pltpu.VMEM((feats, hid), F32),
            pltpu.VMEM((hid, width), F32),
            pltpu.SemaphoreType.DMA((3 + PIECES,)),
        ],
    )(ig, sums)


def solution(mesh):
    both = ("dom", "sub")
    placed = (
        P(both, None),
        P(both, None),
        P(),
        P(),
        P(both, None),
        P(both, None, None),
        P(both, None),
        P(both),
    )
    return jax.shard_map(
        functools.partial(on_device, mesh.shape["dom"], mesh.shape["sub"]),
        mesh=mesh,
        in_specs=placed,
        out_specs=(P(both, None), P(), P()),
        check_vma=False,
    )
```

```python
import functools
import math

import jax
import jax.numpy as jnp
from jax import lax
from jax.experimental import pallas as pl
from jax.experimental.pallas import tpu as pltpu
from jax.sharding import PartitionSpec as P

STEPS = 4
teleport = 0.1
MESH = pl.DeviceIdType.MESH
F32 = jnp.float32
BF16 = jnp.bfloat16
I32 = jnp.int32


def nt_dot(a, b):
    return lax.dot_general(a, b, (((1,), (1,)), ((), ())), preferred_element_type=F32)


def nn_dot(a, b):
    return jnp.dot(a, b, preferred_element_type=F32)


def owner_layout(n_dom, n_sub, grad_rows):
    low = n_sub // 4
    width = n_sub - 2 * low
    chunk = max(8, grad_rows // (n_dom * width))
    return low, width, grad_rows // chunk, chunk


def arrival_groups(n_dom, n_sub):
    half = n_dom // 2
    groups = [[(0, 1, n_dom)]] if n_dom > 1 else []
    for m in reversed(range(3, n_sub)):
        groups += [[(m, 0, half)], [(m, half, n_dom)]] if half else [[(m, 0, n_dom)]]
    left = [m for m in (2, 1) if m < n_sub]
    cuts = sorted({0, half // 2, half, half + half // 2, n_dom - 1, n_dom})
    for start, end in zip(cuts[:-1], cuts[1:]):
        groups.append([(m, start, end) for m in left])
    return [group for group in groups if group]


def kernel(
    n_dom, n_sub, norm_scale,
    list_hbm, count_hbm, up_hbm, tiles_hbm, w_in_hbm, w_out_hbm, adj_hbm, feat_hbm,
    ig_hbm, gfull,
    list_v, count_s, idx_v, idx_s, tiles, w_in, w_out,
    adj, feat, v, outb, arrived, ids_out, ids_in, acc, accum, fac, act_t, feat_t, dpre, ig,
    gsend, gparts, gred,
    local_sem, send_sem, recv_sem, small_sem,
):
    n = n_dom * n_sub
    my_dom, my_sub = lax.axis_index("dom"), lax.axis_index("sub")
    me = my_dom * n_sub + my_sub
    nb, blk, width = v.shape
    rows = nb * blk
    feats, hid = w_in.shape
    tile = min(512, rows)
    blocks = tile // blk
    paired = n_sub & (n_sub - 1) == 0
    pairings = list(reversed(range(n_sub)))
    early = pairings[:-1]
    groups = arrival_groups(n_dom, n_sub)
    group_of = {(m, i): k for k, pieces in enumerate(groups) for m, start, end in pieces for i in range(start, end)}

    def partner(m, sign):
        if not paired:
            return lax.rem(my_sub + sign * m + n_sub, n_sub)
        z, bit = my_sub, 1
        while bit < n_sub:
            if m & bit:
                z = z + bit - 2 * bit * lax.rem(my_sub // bit, 2)
            bit *= 2
        return z

    def peer(m, i, sign=1):
        d = lax.rem(my_dom + sign * i + n_dom, n_dom)
        z = partner(m, sign)
        return d, z, d * n_sub + z

    def each_peer(fn, chosen=None):
        for m in pairings if chosen is None else chosen:
            i = 1 if m == 0 else 0
            while i < n_dom:
                k = group_of[m, i]
                end = i
                while end < n_dom and group_of[m, end] == k:
                    end += 1
                def body(i, carry, m=m, k=k):
                    fn(*peer(m, i), k)
                    return carry
                lax.fori_loop(i, end, body, 0, unroll=m != 0)
                i = end

    barrier = pltpu.get_barrier_semaphore()
    each_peer(lambda d, z, t, k: pl.semaphore_signal(
        barrier, inc=1, device_id=(d, z), device_id_type=MESH))

    loads = [
        pltpu.make_async_copy(src, dst, local_sem.at[i])
        for i, (src, dst) in enumerate([
            (list_hbm, list_v), (count_hbm, count_s), (up_hbm, v), (tiles_hbm, tiles),
            (w_in_hbm, w_in), (w_out_hbm, w_out), (feat_hbm, feat), (adj_hbm, adj)])
    ]
    for load in loads:
        load.start()
    list_load, count_load, up_load, tiles_load, w_in_load, w_out_load, feat_load, adj_load = loads
    list_load.wait()
    count_load.wait()

    entries = list_v.shape[1]
    lanes = idx_v.shape[1]
    first = lax.broadcasted_iota(I32, (n, entries), 0) * nb
    goal = jnp.broadcast_to(list_v[1:2, :], (n, entries))
    live = lax.broadcasted_iota(I32, (n, entries), 1) < count_s[0]
    hit = live & (goal >= first) & (goal < first + nb)

    def pick(values):
        return jnp.sum(jnp.where(hit, values, 0), axis=1, keepdims=True)

    on_diagonal = lax.broadcasted_iota(I32, (n, lanes), 0) == lax.broadcasted_iota(I32, (n, lanes), 1)

    def as_row(column):
        return jnp.sum(jnp.where(on_diagonal, column, 0), axis=0, keepdims=True)

    idx_v[0:1, :] = as_row(pick(list_v[0:1, :]))
    idx_v[1:2, :] = as_row(pick(list_v[2:3, :]))
    idx_copy = pltpu.make_async_copy(idx_v, idx_s, local_sem.at[0])
    idx_copy.start()
    block_id = pick(goal - first - nb) + nb
    ids_out[...] = jnp.broadcast_to(block_id, (n, 128)).reshape(n, 1, 128)
    accum[...] = jnp.zeros_like(accum)

    def id_copy(d, z, t, slot):
        return pltpu.make_async_remote_copy(
            src_ref=ids_out.at[t], dst_ref=ids_in.at[slot], send_sem=small_sem.at[0],
            recv_sem=small_sem.at[1], device_id=(d, z), device_id_type=MESH)

    def block_copy(p, d, z, t, k):
        return pltpu.make_async_remote_copy(
            src_ref=outb.at[p, t], dst_ref=arrived.at[p, me], send_sem=send_sem.at[p],
            recv_sem=recv_sem.at[p, k], device_id=(d, z), device_id_type=MESH)

    def many(ref, count, sem):
        return pltpu.make_async_remote_copy(
            src_ref=ref.at[pl.ds(0, count)], dst_ref=ref.at[pl.ds(0, count)], send_sem=sem,
            recv_sem=sem, device_id=(my_dom, my_sub), device_id_type=MESH)

    def multiply(p, t):
        outb[p, t] = nn_dot(tiles[idx_s[1, t]], v[idx_s[0, t]]).astype(BF16)

    idx_copy.wait()
    up_load.wait()
    tiles_load.wait()
    each_peer(lambda d, z, t, k: multiply(0, t), early)
    pl.semaphore_wait(barrier, n - 1)

    each_peer(lambda d, z, t, k: id_copy(d, z, t, me).start())
    each_peer(lambda d, z, t, k: block_copy(0, d, z, t, k).start(), early)
    late = [m for m in pairings if m not in early]

    for step in range(STEPS):
        p = step % 2

        def send(d, z, t, k):
            multiply(p, t)
            block_copy(p, d, z, t, k).start()

        if step >= 2:
            many(outb.at[p], n - 1, send_sem.at[p]).wait_send()

        each_peer(send, late if step == 0 else pairings)

        if step == 0:
            feat_load.wait()
            w_in_load.wait()
            w_out_load.wait()

            def head(i, carry):
                at = pl.ds(pl.multiple_of(i * tile, tile), tile)
                here = feat[at, :]
                pre = nn_dot(here, w_in[...])
                gate = jax.nn.sigmoid(pre)
                act_t[:, at] = (pre * gate).astype(BF16).T
                feat_t[:, at] = here.T
                fac[at, :] = gate * (1.0 + pre * (1.0 - gate))
                return carry

            lax.fori_loop(0, rows // tile, head, 0)
            adj_load.wait()

        def local(i, carry):
            at = pl.ds(pl.multiple_of(i * tile, tile), tile)
            term = nn_dot(adj[at, :], v[...].reshape(rows, width))
            ats = pl.ds(i * blocks, blocks)
            acc[ats] = term.reshape(blocks, blk, width)
            accum[ats] += teleport * v[ats].astype(F32)
            return carry

        lax.fori_loop(0, rows // tile, local, 0)

        for k, pieces in enumerate(groups):
            last = k == len(groups) - 1
            if step == 0 and k == 0:
                many(ids_in, n - 1, small_sem.at[1]).wait_recv()
            count = sum(end - start for _, start, end in pieces)
            many(arrived.at[p], count, recv_sem.at[p, k]).wait_recv()

            def summed(b):
                total = acc[b]
                for m, start, end in pieces:
                    for i in range(start, end):
                        s = peer(m, i, -1)[2]
                        match = ids_in[s, 0:1, :] == b
                        total += jnp.where(match, arrived[p, s].astype(F32), 0.0)
                return total

            def gather(b, carry):
                if last:
                    v[b] = ((1.0 - teleport) * summed(b)).astype(BF16)
                else:
                    acc[b] = summed(b)
                return carry

            if not (last and step == STEPS - 1):
                lax.fori_loop(0, nb, gather, 0, unroll=4)

    def head_grad(b):
        final = ((1.0 - teleport) * summed(b)).astype(BF16)
        return (accum[b] + final.astype(F32)).astype(BF16)

    low, mid, owners, chunk = owner_layout(n_dom, n_sub, feats + hid)
    split = feats // chunk

    def each_owner(fn, wanted=None):
        for k in range(mid):
            j = jnp.where(my_sub < low + (mid + 1) // 2, mid - 1 - k, k)

            def body(i, carry, j=j):
                d = lax.rem(my_dom + i, n_dom)
                q = d * mid + j
                fit = q < owners if n_dom * mid > owners else None
                other = (i > 0) | (my_sub != low + j)
                other = other if fit is None else other & fit
                pl.when(other if wanted is None else other & wanted(q))(lambda: fn(d, low + j, q))
                return carry
            lax.fori_loop(0, n_dom, body, 0, unroll=True)

    my_chunk = my_dom * mid + my_sub - low
    owning = (my_sub >= low) & (my_sub < low + mid)
    if n_dom * mid > owners:
        owning = owning & (my_chunk < owners)

    def part_copy(d, z, q, slot):
        return pltpu.make_async_remote_copy(
            src_ref=gsend.at[q], dst_ref=gparts.at[slot], send_sem=small_sem.at[2],
            recv_sem=small_sem.at[3], device_id=(d, z), device_id_type=MESH)

    def sum_copy(d, z, q):
        return pltpu.make_async_remote_copy(
            src_ref=gred, dst_ref=gfull.at[q], send_sem=small_sem.at[4],
            recv_sem=small_sem.at[5], device_id=(d, z), device_id_type=MESH)

    def tail_out(i, part_out):
        at = pl.ds(pl.multiple_of(i * tile, tile), tile)
        ats = pl.ds(i * blocks, blocks)
        grad = jnp.concatenate([head_grad(i * blocks + j) for j in range(blocks)], axis=0)
        v[ats] = grad.reshape(blocks, blk, width)
        return part_out + nn_dot(act_t[:, at], grad)

    part_out = lax.fori_loop(0, rows // tile, tail_out, jnp.zeros((hid, width), F32), unroll=True)
    gsend[split:owners] = (part_out * norm_scale).reshape(owners - split, chunk, width).astype(BF16)
    each_owner(lambda d, z, q: part_copy(d, z, q, me).start(), lambda q: q >= split)

    def tail_in(i, part_in):
        at = pl.ds(pl.multiple_of(i * tile, tile), tile)
        ats = pl.ds(i * blocks, blocks)
        back = nt_dot(v[ats].reshape(tile, width), w_out[...])
        inner = (back * fac[at, :]).astype(BF16)
        dpre[at, :] = inner
        return part_in + nn_dot(feat_t[:, at], inner)

    part_in = lax.fori_loop(0, rows // tile, tail_in, jnp.zeros((feats, hid), F32), unroll=True)
    gsend[0:split] = (part_in * norm_scale).reshape(split, chunk, hid).astype(BF16)
    each_owner(lambda d, z, q: part_copy(d, z, q, me).start(), lambda q: q < split)

    def project(i, carry):
        at = pl.ds(pl.multiple_of(i * tile, tile), tile)
        ig[at, :] = nt_dot(dpre[at, :], w_in[...]).astype(BF16)
        return carry

    lax.fori_loop(0, rows // tile, project, 0)
    ig_copy = pltpu.make_async_copy(ig, ig_hbm, local_sem.at[0])
    ig_copy.start()
    many(ids_out, n - 1, small_sem.at[0]).wait_send()
    many(outb.at[0], n - 1, send_sem.at[0]).wait_send()
    many(outb.at[1], n - 1, send_sem.at[1]).wait_send()

    def reduce():
        gparts[me] = gsend[my_chunk]
        many(gparts, n - 1, small_sem.at[3]).wait_recv()
        total = jnp.sum(gparts[...].astype(F32), axis=0).astype(BF16)
        gred[...] = total
        mine = pltpu.make_async_copy(gred, gfull.at[my_chunk], local_sem.at[1])
        mine.start()
        each_peer(lambda d, z, t, k: sum_copy(d, z, my_chunk).start())
        many(gsend, owners - 1, small_sem.at[2]).wait_send()
        many(gfull, owners - 1, small_sem.at[5]).wait_recv()
        many(gparts, n - 1, small_sem.at[4]).wait_send()
        mine.wait()

    def follow():
        many(gsend, owners, small_sem.at[2]).wait_send()
        many(gfull, owners, small_sem.at[5]).wait_recv()

    pl.when(owning)(reduce)
    pl.when(jnp.logical_not(owning))(follow)
    ig_copy.wait()


PIECES = 8


def finish(ig_in, sums_in, ig_out, gin_out, gout_out, ig, sums, gin, gout, sems):
    owners, chunk, _ = sums.shape
    split = gin.shape[0] // chunk
    size = ig.shape[0] // PIECES
    pieces = [pl.ds(i * size, size) for i in range(PIECES)]
    sums_load = pltpu.make_async_copy(sums_in, sums, sems.at[0])
    loads = [pltpu.make_async_copy(ig_in.at[at, :], ig.at[at, :], sems.at[3 + i]) for i, at in enumerate(pieces)]
    stores = [pltpu.make_async_copy(ig.at[at, :], ig_out.at[at, :], sems.at[3 + i]) for i, at in enumerate(pieces)]
    stores += [pltpu.make_async_copy(gin, gin_out, sems.at[1]), pltpu.make_async_copy(gout, gout_out, sems.at[2])]
    sums_load.start()
    for load in loads:
        load.start()
    sums_load.wait()
    gin[...] = sums[0:split].astype(F32).reshape(gin.shape)
    stores[-2].start()
    gout[...] = sums[split:owners].astype(F32).reshape(gout.shape)
    stores[-1].start()
    for load, store in zip(loads, stores):
        load.wait()
        store.start()
    for store in stores:
        store.wait()


def on_device(n_dom, n_sub, upstream, features, w_in, w_out, inner_adj, cut_tiles, cut_list, cut_count):
    n = n_dom * n_sub
    rows, width = upstream.shape
    entries, blk, _ = cut_tiles.shape
    nb = rows // blk
    feats, hid = w_in.shape
    _, _, owners, chunk = owner_layout(n_dom, n_sub, feats + hid)
    lanes = 128 * -(-n // 128)
    vmem = pl.BlockSpec(memory_space=pltpu.VMEM)
    hbm = pl.BlockSpec(memory_space=pl.ANY)
    scratch = [
        pltpu.VMEM((3, entries), I32),
        pltpu.SMEM((1,), I32),
        pltpu.VMEM((2, lanes), I32),
        pltpu.SMEM((2, lanes), I32),
        pltpu.VMEM(cut_tiles.shape, BF16),
        pltpu.VMEM(w_in.shape, BF16),
        pltpu.VMEM(w_out.shape, BF16),
        pltpu.VMEM(inner_adj.shape, BF16),
        pltpu.VMEM(features.shape, BF16),
        pltpu.VMEM((nb, blk, width), BF16),
        pltpu.VMEM((2, n, blk, width), BF16),
        pltpu.VMEM((2, n, blk, width), BF16),
        pltpu.VMEM((n, 1, 128), I32),
        pltpu.VMEM((n, 1, 128), I32),
        pltpu.VMEM((nb, blk, width), F32),
        pltpu.VMEM((nb, blk, width), F32),
        pltpu.VMEM((rows, hid), F32),
        pltpu.VMEM((hid, rows), BF16),
        pltpu.VMEM((feats, rows), BF16),
        pltpu.VMEM((rows, hid), BF16),
        pltpu.VMEM((rows, feats), BF16),
        pltpu.VMEM((owners, chunk, hid), BF16),
        pltpu.VMEM((n, chunk, hid), BF16),
        pltpu.VMEM((chunk, hid), BF16),
        pltpu.SemaphoreType.DMA((8,)),
        pltpu.SemaphoreType.DMA((2,)),
        pltpu.SemaphoreType.DMA((2, len(arrival_groups(n_dom, n_sub)))),
        pltpu.SemaphoreType.DMA((6,)),
    ]
    ig, sums = pl.pallas_call(
        functools.partial(kernel, n_dom, n_sub, 1.0 / math.sqrt(rows * n)),
        out_shape=(
            jax.ShapeDtypeStruct((rows, feats), BF16),
            jax.ShapeDtypeStruct((owners, chunk, hid), BF16),
        ),
        in_specs=[hbm] * 8,
        out_specs=(hbm, hbm),
        scratch_shapes=scratch,
        compiler_params=pltpu.CompilerParams(collective_id=0, has_side_effects=True),
    )(cut_list.T, cut_count, upstream.reshape(nb, blk, width), cut_tiles, w_in, w_out, inner_adj, features)
    return pl.pallas_call(
        finish,
        out_shape=(
            jax.ShapeDtypeStruct((rows, feats), BF16),
            jax.ShapeDtypeStruct((feats, hid), F32),
            jax.ShapeDtypeStruct((hid, width), F32),
        ),
        in_specs=[hbm, hbm],
        out_specs=(hbm, hbm, hbm),
        scratch_shapes=[
            pltpu.VMEM((rows, feats), BF16),
            pltpu.VMEM(sums.shape, BF16),
            pltpu.VMEM((feats, hid), F32),
            pltpu.VMEM((hid, width), F32),
            pltpu.SemaphoreType.DMA((3 + PIECES,)),
        ],
    )(ig, sums)


def solution(mesh):
    both = ("dom", "sub")
    placed = (
        P(both, None),
        P(both, None),
        P(),
        P(),
        P(both, None),
        P(both, None, None),
        P(both, None),
        P(both),
    )
    return jax.shard_map(
        functools.partial(on_device, mesh.shape["dom"], mesh.shape["sub"]),
        mesh=mesh,
        in_specs=placed,
        out_specs=(P(both, None), P(), P()),
        check_vma=False,
    )
```

```python
import functools
import math

import jax
import jax.numpy as jnp
from jax import lax
from jax.experimental import pallas as pl
from jax.experimental.pallas import tpu as pltpu
from jax.sharding import PartitionSpec as P

STEPS = 4
teleport = 0.1
MESH = pl.DeviceIdType.MESH
F32 = jnp.float32
BF16 = jnp.bfloat16
I32 = jnp.int32


def nn_dot(a, b):
    return jnp.dot(a, b, preferred_element_type=F32)


def owner_layout(n_dom, n_sub, grad_rows):
    low = n_sub // 4
    width = n_sub - 2 * low
    chunk = max(8, grad_rows // (n_dom * width))
    return low, width, grad_rows // chunk, chunk


def arrival_groups(n_dom, n_sub):
    half = n_dom // 2
    groups = [[(0, 1, n_dom)]] if n_dom > 1 else []
    for m in reversed(range(3, n_sub)):
        groups += [[(m, 0, half)], [(m, half, n_dom)]] if half else [[(m, 0, n_dom)]]
    left = [m for m in (2, 1) if m < n_sub]
    cuts = sorted({0, half, half + half // 2, n_dom - 1, n_dom})
    for start, end in zip(cuts[:-1], cuts[1:]):
        if end == n_dom:
            groups.append([(m, start, end) for m in left])
        else:
            groups += [[(m, start, end)] for m in left]
    return [group for group in groups if group]


def kernel(
    n_dom, n_sub, norm_scale,
    list_hbm, count_hbm, up_hbm, tiles_hbm, w_in_hbm, w_out_hbm, adj_hbm, feat_hbm,
    ig_hbm, gfull,
    list_v, count_s, idx_v, idx_s, tiles, w_in, w_out, w_in_t, w_out_t,
    adj, feat, v, outb, arrived, ids_out, ids_in, acc, accum, fac, act_t, feat_t, dpre, ig,
    gsend, gparts, gred,
    local_sem, send_sem, recv_sem, small_sem,
):
    n = n_dom * n_sub
    my_dom, my_sub = lax.axis_index("dom"), lax.axis_index("sub")
    me = my_dom * n_sub + my_sub
    nb, blk, width = v.shape
    rows = nb * blk
    feats, hid = w_in.shape
    tile = min(512, rows)
    blocks = tile // blk
    paired = n_sub & (n_sub - 1) == 0
    pairings = list(reversed(range(n_sub)))
    early = pairings[: n_sub // 2] if n_sub > 1 else []
    groups = arrival_groups(n_dom, n_sub)
    group_of = {(m, i): k for k, pieces in enumerate(groups) for m, start, end in pieces for i in range(start, end)}

    def partner(m, sign):
        if not paired:
            return lax.rem(my_sub + sign * m + n_sub, n_sub)
        z, bit = my_sub, 1
        while bit < n_sub:
            if m & bit:
                z = z + bit - 2 * bit * lax.rem(my_sub // bit, 2)
            bit *= 2
        return z

    def peer(m, i, sign=1):
        d = lax.rem(my_dom + sign * i + n_dom, n_dom)
        z = partner(m, sign)
        return d, z, d * n_sub + z

    def each_peer(fn, chosen=None):
        for m in pairings if chosen is None else chosen:
            i = 1 if m == 0 else 0
            while i < n_dom:
                k = group_of[m, i]
                end = i
                while end < n_dom and group_of[m, end] == k:
                    end += 1
                def body(i, carry, m=m, k=k):
                    fn(*peer(m, i), k)
                    return carry
                lax.fori_loop(i, end, body, 0, unroll=m != 0)
                i = end

    barrier = pltpu.get_barrier_semaphore()
    each_peer(lambda d, z, t, k: pl.semaphore_signal(
        barrier, inc=1, device_id=(d, z), device_id_type=MESH))

    loads = [
        pltpu.make_async_copy(src, dst, local_sem.at[i])
        for i, (src, dst) in enumerate([
            (list_hbm, list_v), (count_hbm, count_s), (up_hbm, v), (tiles_hbm, tiles),
            (w_in_hbm, w_in), (w_out_hbm, w_out), (feat_hbm, feat), (adj_hbm, adj)])
    ]
    for load in loads:
        load.start()
    list_load, count_load, up_load, tiles_load, w_in_load, w_out_load, feat_load, adj_load = loads
    list_load.wait()
    count_load.wait()

    entries = list_v.shape[1]
    lanes = idx_v.shape[1]
    first = lax.broadcasted_iota(I32, (n, entries), 0) * nb
    goal = jnp.broadcast_to(list_v[1:2, :], (n, entries))
    live = lax.broadcasted_iota(I32, (n, entries), 1) < count_s[0]
    hit = live & (goal >= first) & (goal < first + nb)

    def pick(values):
        return jnp.sum(jnp.where(hit, values, 0), axis=1, keepdims=True)

    on_diagonal = lax.broadcasted_iota(I32, (n, lanes), 0) == lax.broadcasted_iota(I32, (n, lanes), 1)

    def as_row(column):
        return jnp.sum(jnp.where(on_diagonal, column, 0), axis=0, keepdims=True)

    idx_v[0:1, :] = as_row(pick(list_v[0:1, :]))
    idx_v[1:2, :] = as_row(pick(list_v[2:3, :]))
    idx_copy = pltpu.make_async_copy(idx_v, idx_s, local_sem.at[0])
    idx_copy.start()
    block_id = pick(goal - first - nb) + nb
    ids_out[...] = jnp.broadcast_to(block_id, (n, 128)).reshape(n, 1, 128)
    accum[...] = jnp.zeros_like(accum)

    def id_copy(d, z, t, slot):
        return pltpu.make_async_remote_copy(
            src_ref=ids_out.at[t], dst_ref=ids_in.at[slot], send_sem=small_sem.at[0],
            recv_sem=small_sem.at[1], device_id=(d, z), device_id_type=MESH)

    def block_copy(p, d, z, t, k):
        return pltpu.make_async_remote_copy(
            src_ref=outb.at[p, t], dst_ref=arrived.at[p, me], send_sem=send_sem.at[p],
            recv_sem=recv_sem.at[p, k], device_id=(d, z), device_id_type=MESH)

    def many(ref, count, sem):
        return pltpu.make_async_remote_copy(
            src_ref=ref.at[pl.ds(0, count)], dst_ref=ref.at[pl.ds(0, count)], send_sem=sem,
            recv_sem=sem, device_id=(my_dom, my_sub), device_id_type=MESH)

    def multiply(p, t):
        outb[p, t] = nn_dot(tiles[idx_s[1, t]], v[idx_s[0, t]]).astype(BF16)

    idx_copy.wait()
    up_load.wait()
    tiles_load.wait()
    each_peer(lambda d, z, t, k: multiply(0, t), early)
    pl.semaphore_wait(barrier, n - 1)

    each_peer(lambda d, z, t, k: id_copy(d, z, t, me).start())
    each_peer(lambda d, z, t, k: block_copy(0, d, z, t, k).start(), early)
    late = [m for m in pairings if m not in early]

    for step in range(STEPS):
        p = step % 2

        def send(d, z, t, k):
            multiply(p, t)
            block_copy(p, d, z, t, k).start()

        if step >= 2:
            many(outb.at[p], n - 1, send_sem.at[p]).wait_send()

        each_peer(send, late if step == 0 else pairings)

        if step == 0:
            feat_load.wait()
            w_in_load.wait()
            w_out_load.wait()
            w_out_t[...] = w_out[...].T
            w_in_t[...] = w_in[...].T

            def head(i, carry):
                at = pl.ds(pl.multiple_of(i * tile, tile), tile)
                here = feat[at, :]
                pre = nn_dot(here, w_in[...])
                gate = jax.nn.sigmoid(pre)
                act_t[:, at] = (pre * gate).astype(BF16).T
                feat_t[:, at] = here.T
                fac[at, :] = gate * (1.0 + pre * (1.0 - gate))
                return carry

            lax.fori_loop(0, rows // tile, head, 0)
            adj_load.wait()

        def local(i, carry):
            at = pl.ds(pl.multiple_of(i * tile, tile), tile)
            term = nn_dot(adj[at, :], v[...].reshape(rows, width))
            ats = pl.ds(i * blocks, blocks)
            acc[ats] = term.reshape(blocks, blk, width)
            accum[ats] += teleport * v[ats].astype(F32)
            return carry

        lax.fori_loop(0, rows // tile, local, 0)

        for k, pieces in enumerate(groups):
            last = k == len(groups) - 1
            if step == 0 and k == 0:
                many(ids_in, n - 1, small_sem.at[1]).wait_recv()
            count = sum(end - start for _, start, end in pieces)
            many(arrived.at[p], count, recv_sem.at[p, k]).wait_recv()

            def summed(b):
                total = acc[b]
                for m, start, end in pieces:
                    for i in range(start, end):
                        s = peer(m, i, -1)[2]
                        match = ids_in[s, 0:1, :] == b
                        total += jnp.where(match, arrived[p, s].astype(F32), 0.0)
                return total

            def gather(b, carry):
                if last:
                    v[b] = ((1.0 - teleport) * summed(b)).astype(BF16)
                else:
                    acc[b] = summed(b)
                return carry

            if not (last and step == STEPS - 1):
                lax.fori_loop(0, nb, gather, 0, unroll=4)

    def head_grad(b):
        final = ((1.0 - teleport) * summed(b)).astype(BF16)
        return (accum[b] + final.astype(F32)).astype(BF16)

    low, mid, owners, chunk = owner_layout(n_dom, n_sub, feats + hid)
    split = feats // chunk

    def each_owner(fn, wanted=None):
        for k in range(mid):
            j = jnp.where(my_sub < low + (mid + 1) // 2, mid - 1 - k, k)

            def body(i, carry, j=j):
                d = lax.rem(my_dom + i, n_dom)
                q = d * mid + j
                fit = q < owners if n_dom * mid > owners else None
                other = (i > 0) | (my_sub != low + j)
                other = other if fit is None else other & fit
                pl.when(other if wanted is None else other & wanted(q))(lambda: fn(d, low + j, q))
                return carry
            lax.fori_loop(0, n_dom, body, 0)

    my_chunk = my_dom * mid + my_sub - low
    owning = (my_sub >= low) & (my_sub < low + mid)
    if n_dom * mid > owners:
        owning = owning & (my_chunk < owners)

    def part_copy(d, z, q, slot):
        return pltpu.make_async_remote_copy(
            src_ref=gsend.at[q], dst_ref=gparts.at[slot], send_sem=small_sem.at[2],
            recv_sem=small_sem.at[3], device_id=(d, z), device_id_type=MESH)

    def sum_copy(d, z, q):
        return pltpu.make_async_remote_copy(
            src_ref=gred, dst_ref=gfull.at[q], send_sem=small_sem.at[4],
            recv_sem=small_sem.at[5], device_id=(d, z), device_id_type=MESH)

    def tail_out(i, part_out):
        at = pl.ds(pl.multiple_of(i * tile, tile), tile)
        ats = pl.ds(i * blocks, blocks)
        grad = jnp.concatenate([head_grad(i * blocks + j) for j in range(blocks)], axis=0)
        v[ats] = grad.reshape(blocks, blk, width)
        return part_out + nn_dot(act_t[:, at], grad)

    part_out = lax.fori_loop(0, rows // tile, tail_out, jnp.zeros((hid, width), F32), unroll=True)
    gsend[split:owners] = (part_out * norm_scale).reshape(owners - split, chunk, width).astype(BF16)
    each_owner(lambda d, z, q: part_copy(d, z, q, me).start(), lambda q: q >= split)

    def tail_in(i, part_in):
        at = pl.ds(pl.multiple_of(i * tile, tile), tile)
        ats = pl.ds(i * blocks, blocks)
        back = nn_dot(v[ats].reshape(tile, width), w_out_t[...])
        inner = (back * fac[at, :]).astype(BF16)
        dpre[at, :] = inner
        return part_in + nn_dot(feat_t[:, at], inner)

    part_in = lax.fori_loop(0, rows // tile, tail_in, jnp.zeros((feats, hid), F32), unroll=True)
    gsend[0:split] = (part_in * norm_scale).reshape(split, chunk, hid).astype(BF16)
    each_owner(lambda d, z, q: part_copy(d, z, q, me).start(), lambda q: q < split)

    def project(i, carry):
        at = pl.ds(pl.multiple_of(i * tile, tile), tile)
        ig[at, :] = nn_dot(dpre[at, :], w_in_t[...]).astype(BF16)
        return carry

    lax.fori_loop(0, rows // tile, project, 0)
    ig_copy = pltpu.make_async_copy(ig, ig_hbm, local_sem.at[0])
    ig_copy.start()
    many(ids_out, n - 1, small_sem.at[0]).wait_send()
    many(outb.at[0], n - 1, send_sem.at[0]).wait_send()
    many(outb.at[1], n - 1, send_sem.at[1]).wait_send()

    def reduce():
        gparts[me] = gsend[my_chunk]
        many(gparts, n - 1, small_sem.at[3]).wait_recv()
        total = jnp.sum(gparts[...].astype(F32), axis=0).astype(BF16)
        gred[...] = total
        mine = pltpu.make_async_copy(gred, gfull.at[my_chunk], local_sem.at[1])
        mine.start()
        each_peer(lambda d, z, t, k: sum_copy(d, z, my_chunk).start())
        many(gsend, owners - 1, small_sem.at[2]).wait_send()
        many(gfull, owners - 1, small_sem.at[5]).wait_recv()
        many(gparts, n - 1, small_sem.at[4]).wait_send()
        mine.wait()

    def follow():
        many(gsend, owners, small_sem.at[2]).wait_send()
        many(gfull, owners, small_sem.at[5]).wait_recv()

    pl.when(owning)(reduce)
    pl.when(jnp.logical_not(owning))(follow)
    ig_copy.wait()


PIECES = 8


def finish(ig_in, sums_in, ig_out, gin_out, gout_out, ig, sums, gin, gout, sems):
    owners, chunk, _ = sums.shape
    split = gin.shape[0] // chunk
    size = ig.shape[0] // PIECES
    pieces = [pl.ds(i * size, size) for i in range(PIECES)]
    sums_load = pltpu.make_async_copy(sums_in, sums, sems.at[0])
    loads = [pltpu.make_async_copy(ig_in.at[at, :], ig.at[at, :], sems.at[3 + i]) for i, at in enumerate(pieces)]
    stores = [pltpu.make_async_copy(ig.at[at, :], ig_out.at[at, :], sems.at[3 + i]) for i, at in enumerate(pieces)]
    stores += [pltpu.make_async_copy(gin, gin_out, sems.at[1]), pltpu.make_async_copy(gout, gout_out, sems.at[2])]
    sums_load.start()
    for load in loads:
        load.start()
    sums_load.wait()
    gin[...] = sums[0:split].astype(F32).reshape(gin.shape)
    stores[-2].start()
    gout[...] = sums[split:owners].astype(F32).reshape(gout.shape)
    stores[-1].start()
    for load, store in zip(loads, stores):
        load.wait()
        store.start()
    for store in stores:
        store.wait()


def on_device(n_dom, n_sub, upstream, features, w_in, w_out, inner_adj, cut_tiles, cut_list, cut_count):
    n = n_dom * n_sub
    rows, width = upstream.shape
    entries, blk, _ = cut_tiles.shape
    nb = rows // blk
    feats, hid = w_in.shape
    _, _, owners, chunk = owner_layout(n_dom, n_sub, feats + hid)
    lanes = 128 * -(-n // 128)
    vmem = pl.BlockSpec(memory_space=pltpu.VMEM)
    hbm = pl.BlockSpec(memory_space=pl.ANY)
    scratch = [
        pltpu.VMEM((3, entries), I32),
        pltpu.SMEM((1,), I32),
        pltpu.VMEM((2, lanes), I32),
        pltpu.SMEM((2, lanes), I32),
        pltpu.VMEM(cut_tiles.shape, BF16),
        pltpu.VMEM(w_in.shape, BF16),
        pltpu.VMEM(w_out.shape, BF16),
        pltpu.VMEM(w_in.shape[::-1], BF16),
        pltpu.VMEM(w_out.shape[::-1], BF16),
        pltpu.VMEM(inner_adj.shape, BF16),
        pltpu.VMEM(features.shape, BF16),
        pltpu.VMEM((nb, blk, width), BF16),
        pltpu.VMEM((2, n, blk, width), BF16),
        pltpu.VMEM((2, n, blk, width), BF16),
        pltpu.VMEM((n, 1, 128), I32),
        pltpu.VMEM((n, 1, 128), I32),
        pltpu.VMEM((nb, blk, width), F32),
        pltpu.VMEM((nb, blk, width), F32),
        pltpu.VMEM((rows, hid), F32),
        pltpu.VMEM((hid, rows), BF16),
        pltpu.VMEM((feats, rows), BF16),
        pltpu.VMEM((rows, hid), BF16),
        pltpu.VMEM((rows, feats), BF16),
        pltpu.VMEM((owners, chunk, hid), BF16),
        pltpu.VMEM((n, chunk, hid), BF16),
        pltpu.VMEM((chunk, hid), BF16),
        pltpu.SemaphoreType.DMA((8,)),
        pltpu.SemaphoreType.DMA((2,)),
        pltpu.SemaphoreType.DMA((2, len(arrival_groups(n_dom, n_sub)))),
        pltpu.SemaphoreType.DMA((6,)),
    ]
    ig, sums = pl.pallas_call(
        functools.partial(kernel, n_dom, n_sub, 1.0 / math.sqrt(rows * n)),
        out_shape=(
            jax.ShapeDtypeStruct((rows, feats), BF16),
            jax.ShapeDtypeStruct((owners, chunk, hid), BF16),
        ),
        in_specs=[hbm] * 8,
        out_specs=(hbm, hbm),
        scratch_shapes=scratch,
        compiler_params=pltpu.CompilerParams(collective_id=0, has_side_effects=True),
    )(cut_list.T, cut_count, upstream.reshape(nb, blk, width), cut_tiles, w_in, w_out, inner_adj, features)
    return pl.pallas_call(
        finish,
        out_shape=(
            jax.ShapeDtypeStruct((rows, feats), BF16),
            jax.ShapeDtypeStruct((feats, hid), F32),
            jax.ShapeDtypeStruct((hid, width), F32),
        ),
        in_specs=[hbm, hbm],
        out_specs=(hbm, hbm, hbm),
        scratch_shapes=[
            pltpu.VMEM((rows, feats), BF16),
            pltpu.VMEM(sums.shape, BF16),
            pltpu.VMEM((feats, hid), F32),
            pltpu.VMEM((hid, width), F32),
            pltpu.SemaphoreType.DMA((3 + PIECES,)),
        ],
    )(ig, sums)


def solution(mesh):
    both = ("dom", "sub")
    placed = (
        P(both, None),
        P(both, None),
        P(),
        P(),
        P(both, None),
        P(both, None, None),
        P(both, None),
        P(both),
    )
    return jax.shard_map(
        functools.partial(on_device, mesh.shape["dom"], mesh.shape["sub"]),
        mesh=mesh,
        in_specs=placed,
        out_specs=(P(both, None), P(), P()),
        check_vma=False,
    )
```
